512 devices in a mesh: rows: 64 (over x, z_lo, core), cols: 8 (over y, z_hi).
Axes of the slice: x: 4, y: 4, z: 16 (z_hi: 2, z_lo: 8; z = z_hi * 8 + z_lo), core: 2. Of those that a mesh axis runs over, the one named last changes fastest.
Arguments:
- features: bfloat16 [786432, 256], P(('rows', 'cols')), may hold values from -6 to 6
- adj_values: bfloat16 [6144, 3, 128, 128], P(('rows', 'cols')), may hold values from -0.3125 to 0.3125
- adj_offset: int32 [6144, 3], P(('rows', 'cols')), may hold values from -2 to 2, as said below
- adj_count: int32 [6144], P(('rows', 'cols')), may hold values from 1 to 3, as said below
- weight: bfloat16 [256, 256], replicated, may hold values from -0.375 to 0.375
- bias_vector: float32 [256], replicated, may hold values from -4 to 4
- cotangent: bfloat16 [786432, 256], P(('rows', 'cols')), may hold values from -6 to 6
Outputs:
- activated: bfloat16 [786432, 256], P(('rows', 'cols'))
- grad_features: bfloat16 [786432, 256], P(('rows', 'cols'))
- grad_weight: float32 [256, 256], replicated
- grad_bias: float32 [256], replicated
The draws below stay inside these ranges and needn't reach their ends.
Inputs may be any that keep to these rules, and one draw needn't show every extreme that they name: Slot 0 of every row block has offset 0; the offsets of one row block are distinct, and for row block i every i + adj_offset[i, s] lies in 0 to 6143. Row block i uses its slots 0 to adj_count[i] - 1; the values and offsets of its other slots are ignored. In every draw all row blocks of one device, drawn from the seed, use all 3 slots.
All inputs are finite; a program needn't handle non-finite values.
Results may differ from the reference program's by a relative error of at most 0.0075.
Values may be sent and summed in bfloat16 or wider, within the bound.
A program may use at most 64 MiB of HBM per device.

```python
import math
import jax
import jax.numpy as jnp
from jax import lax

F = 256
BLK = 128
BAND = 2
ROW_SLOTS = 3
BLK_DEV = 12
NBLK = 6144
NODES = 786432


def draw_adj_offset(key, part):
    candidates = jnp.concatenate([jnp.arange(-BAND, 0, dtype=jnp.int32), jnp.arange(1, BAND + 1, dtype=jnp.int32)])
    row_index = jnp.arange(NBLK, dtype=jnp.int32)[:, None]
    landing = row_index + candidates[None, :]
    inside = (landing >= 0) & (landing < NBLK)
    scores = jax.random.randint(jax.random.fold_in(key, 11), (NBLK, 2 * BAND), 0, 1 << 20) * (2 * BAND)
    scores = scores + jnp.arange(2 * BAND, dtype=jnp.int32)[None, :]
    scores = scores + jnp.where(inside, 1 << 26, 0).astype(jnp.int32)
    unused_scores, chosen = lax.top_k(scores, ROW_SLOTS - 1)
    picked = candidates[chosen]
    return jnp.concatenate([jnp.zeros((NBLK, 1), jnp.int32), picked], 1).astype(jnp.int32)


def draw_adj_count(key, part):
    base_count = jax.random.randint(jax.random.fold_in(key, 21), (NBLK,), 1, ROW_SLOTS + 1)
    busiest = jax.random.randint(jax.random.fold_in(key, 22), (), 0, NBLK // BLK_DEV)
    owner = jnp.arange(NBLK, dtype=jnp.int32) // BLK_DEV
    return jnp.where(owner == busiest, ROW_SLOTS, base_count).astype(jnp.int32)


def steps_of(rng, extent, split, smallest, largest):
    loudness, own = 1.0, jax.random.fold_in(rng, 6)
    for dim, shards_of in split:
        heights = jnp.exp(jax.random.uniform(jax.random.fold_in(own, dim), (shards_of,), jnp.float32, smallest / len(split), largest / len(split)))
        loudness = loudness * jnp.repeat(heights, extent[dim] // shards_of).reshape([-1 if axis == dim else 1 for axis in range(len(extent))])
    return loudness


def gaussian(own_key, shape, scale, reach, cuts=(), kind=jnp.bfloat16):
    entries = scale * jax.random.normal(own_key, shape, jnp.float32)
    if cuts:
        entries = entries * steps_of(own_key, shape, cuts, -0.22, 0.18)
    return jnp.clip(entries, -reach, reach).astype(kind)


def setup_inputs(seed: int = 0) -> dict:
    keys = jax.random.split(jax.random.key(seed), 8)
    features = gaussian(keys[0], (NODES, F), 1.0, 6.0, ((0, 512),))
    adj_values = gaussian(keys[1], (NBLK, ROW_SLOTS, BLK, BLK), (BLK * ROW_SLOTS) ** -0.5, 0.3125, ((0, 512),))
    adj_offset = draw_adj_offset(jax.random.fold_in(keys[7], 71), 0)
    adj_count = draw_adj_count(jax.random.fold_in(keys[7], 71), 0)
    weight = gaussian(keys[4], (F, F), F ** -0.5, 0.375)
    bias_vector = gaussian(keys[5], (F,), 1.0, 4.0, (), jnp.float32)
    cotangent = gaussian(keys[6], (NODES, F), 1.0, 6.0, ((0, 512),))
    return dict(features=features, adj_values=adj_values, adj_offset=adj_offset, adj_count=adj_count, weight=weight, bias_vector=bias_vector, cotangent=cotangent)


def reference(features, adj_values, adj_offset, adj_count, weight, bias_vector, cotangent):
    group_total = NBLK // BLK_DEV
    span_blocks = BLK_DEV + 2 * BAND
    feat_blocks = features.reshape(NBLK, BLK, F)
    border = jnp.zeros((BAND, BLK, F), features.dtype)
    padded = jnp.concatenate([border, feat_blocks, border], 0)
    values_grouped = adj_values.reshape(group_total, BLK_DEV, ROW_SLOTS, BLK, BLK)
    offset_grouped = adj_offset.reshape(group_total, BLK_DEV, ROW_SLOTS)
    count_grouped = adj_count.reshape(group_total, BLK_DEV)
    slot_index = jnp.arange(ROW_SLOTS, dtype=jnp.int32)
    block_index = jnp.arange(BLK_DEV, dtype=jnp.int32)
    group_ids = jnp.arange(group_total, dtype=jnp.int32)

    def aggregate(inputs):
        group, values, offsets, counts = inputs
        window = lax.dynamic_slice_in_dim(padded, (group * BLK_DEV).astype(jnp.int32), span_blocks, 0)
        target = block_index[:, None] + BAND + offsets
        active = slot_index[None, :] < counts[:, None]
        picked = window[target]
        picked = jnp.where(active[:, :, None, None], picked, jnp.zeros_like(picked))
        return jnp.einsum('bsac,bscf->baf', values.astype(jnp.float32), picked.astype(jnp.float32))
    summed = lax.map(aggregate, (group_ids, values_grouped, offset_grouped, count_grouped))
    aggregated = summed.reshape(NODES, F).astype(jnp.bfloat16)
    preact = jnp.dot(aggregated, weight, preferred_element_type=jnp.float32) + bias_vector
    activated = jax.nn.silu(preact).astype(jnp.bfloat16)
    sigmoid_pre = jax.nn.sigmoid(preact)
    grad_pre = (cotangent.astype(jnp.float32) * sigmoid_pre * (1.0 + preact * (1.0 - sigmoid_pre))).astype(jnp.bfloat16)
    norm_scale = 1.0 / math.sqrt(NODES)
    grad_weight = jnp.dot(aggregated.T, grad_pre, preferred_element_type=jnp.float32) * norm_scale
    grad_bias = lax.optimization_barrier(jnp.sum(grad_pre.astype(jnp.float32), axis=0)) * norm_scale
    upstream = jnp.dot(grad_pre, weight.T, preferred_element_type=jnp.float32).astype(jnp.bfloat16)
    upstream_grouped = upstream.reshape(group_total, BLK_DEV, BLK, F)

    def spread(inputs):
        values, offsets, counts, grads = inputs
        target = block_index[:, None] + BAND + offsets
        active = slot_index[None, :] < counts[:, None]
        slot_terms = jnp.einsum('bsac,baf->bscf', values.astype(jnp.float32), grads.astype(jnp.float32))
        slot_terms = jnp.where(active[:, :, None, None], slot_terms, jnp.zeros_like(slot_terms))
        empty = jnp.zeros((span_blocks, BLK, F), jnp.float32)
        return empty.at[target.reshape(-1)].add(slot_terms.reshape(-1, BLK, F))

    def advance(carry, inputs):
        pending, upper_prev = carry
        extended = spread(inputs)
        lower_part = extended[:BAND]
        middle = extended[BAND:BAND + BLK_DEV]
        upper_part = extended[BAND + BLK_DEV:]
        finished = pending.at[BLK_DEV - BAND:].add(lower_part)
        pending_next = middle.at[:BAND].add(upper_prev)
        return ((pending_next, upper_part), finished)
    start_state = (jnp.zeros((BLK_DEV, BLK, F), jnp.float32), jnp.zeros((BAND, BLK, F), jnp.float32))
    (last_pending, upper_last), finished = lax.scan(advance, start_state, (values_grouped, offset_grouped, count_grouped, upstream_grouped))
    grad_blocks = jnp.concatenate([finished[1:], last_pending[None]], 0)
    grad_features = grad_blocks.reshape(NODES, F).astype(jnp.bfloat16)
    return (activated, grad_features, grad_weight, grad_bias)
```

```python
import math

import jax
import jax.numpy as jnp
from jax import lax
from jax.experimental import pallas as pl
from jax.experimental.pallas import tpu as pltpu
from jax.sharding import PartitionSpec as P

MESH = pl.DeviceIdType.MESH
F32 = jnp.float32
BF16 = jnp.bfloat16
BLK = 128
PAIR = 256
PAIRS = 6
SLOTS = 3
PLANE = 16
PIECE = 16


def dot(a, b):
    return jnp.dot(a, b, preferred_element_type=F32)


def dot_t(a, b):
    return lax.dot_general(a, b, (((0,), (0,)), ((), ())), preferred_element_type=F32)


def place():
    rows, cols = lax.axis_index("rows"), lax.axis_index("cols")
    return rows // 16, cols // 2, (cols % 2) * 8 + (rows // 2) % 8, rows % 2


def device(x, y, z, core):
    return ((x * 8 + z % 8) * 2 + core, y * 2 + z // 8)


def along(step):
    flat = (lax.axis_index("rows") * 8 + lax.axis_index("cols") + step + 512) % 512
    return (flat // 8, flat % 8)


def kernel(
    norm_scale,
    feat_hbm, adj_hbm, off_ref, cnt_ref, w_ref, bias_ref, cot_hbm,
    act_hbm, gf_hbm, gw_ref, gb_ref,
    x_ref, a_ref, cot_ref, tile_ref, edge_acc, u_ref, act_ref, gf_ref, gf_acc, gf_edge,
    halo, spill, landed, grad_half, bias_acc,
    from_core, plane_out, plane_in, z_near, z_far, full_half, other_half,
    load_sem, save_sem, halo_send, halo_recv, spill_send, spill_recv,
    core_send, core_recv, plane_send, plane_recv, near_send, near_recv, far_send, far_recv,
    gather_send, gather_recv, back_send, back_recv,
):
    x, y, z, core = place()
    mine = x * 4 + y
    group, member = z // 4, z % 4

    def plane_peer(step):
        j = (mine + step) % PLANE
        return j, device(j // 4, j % 4, z, core)

    def near_peer(step):
        m = (member + step) % 4
        return device(x, y, group * 4 + m, core)

    def far_peer(step):
        g = (group + step) % 4
        return device(x, y, g * 4 + member, core)

    other_core = device(x, y, z, 1 - core)

    entry = pltpu.get_barrier_semaphore()

    def greet(target):
        pl.semaphore_signal(entry, inc=1, device_id=target, device_id_type=MESH)

    greet(along(1))
    greet(along(-1))
    for step in range(1, 4):
        greet(far_peer(step))
    for step in range(1, PLANE):
        greet(plane_peer(step)[1])
    for step in range(1, 4):
        greet(near_peer(step))
    greet(other_core)

    loads = [
        pltpu.make_async_copy(adj_hbm, a_ref.at[pl.ds(0, 2 * PAIRS)], load_sem.at[0]),
        pltpu.make_async_copy(feat_hbm, x_ref, load_sem.at[1]),
        pltpu.make_async_copy(cot_hbm, cot_ref, load_sem.at[2]),
    ]
    for load in loads:
        load.start()
    for s in range(SLOTS):
        a_ref[2 * PAIRS, s] = jnp.zeros((BLK, BLK), BF16)
    bias_acc[...] = jnp.zeros_like(bias_acc)
    grad_half[...] = jnp.zeros_like(grad_half)
    loads[0].wait()

    def build(p, carry):
        for r in range(2):
            i = 2 * p + r
            count = cnt_ref[i]
            offs = [off_ref[i, s] for s in range(SLOTS)]
            for q in range(3):
                for c in range(2):
                    k = 2 * (q - 1) + c - r
                    at = (pl.ds(r * BLK, BLK), pl.ds(c * BLK, BLK))
                    if abs(k) > 2:
                        tile_ref[p, q, at[0], at[1]] = jnp.zeros((BLK, BLK), BF16)
                        continue
                    row, slot = jnp.int32(2 * PAIRS), jnp.int32(0)
                    for s in range(SLOTS):
                        hit = jnp.logical_and(offs[s] == k, s < count)
                        row = jnp.where(hit, i, row)
                        slot = jnp.where(hit, s, slot)
                    tile_ref[p, q, at[0], at[1]] = a_ref[row, slot]
        return carry

    lax.fori_loop(0, PAIRS, build, 0)
    loads[1].wait()
    loads[2].wait()

    def layer(p, summed):
        rows = pl.ds(pl.multiple_of(p * PAIR, PAIR), PAIR)
        agg = summed.astype(BF16)
        pre = dot(agg, w_ref[...]) + bias_ref[...]
        q = jax.nn.sigmoid(pre)
        act_ref[rows, :] = (pre * q).astype(BF16)
        grad_pre = (cot_ref[rows, :].astype(F32) * q * (1.0 + pre * (1.0 - q))).astype(BF16)
        up = lax.dot_general(
            grad_pre, w_ref[...], (((1,), (1,)), ((), ())), preferred_element_type=F32
        ).astype(BF16)
        u_ref[p] = up
        gw = dot_t(agg, grad_pre)
        grad_half[0, pl.ds(0, PAIR)] += gw[:, :BLK]
        grad_half[1, pl.ds(0, PAIR)] += gw[:, BLK:]
        bias_acc[...] += jnp.sum(grad_pre.astype(F32).reshape(PAIR // 8, 8, PAIR), axis=0)

    def x_pair(p):
        return x_ref[pl.ds(pl.multiple_of(p * PAIR, PAIR), PAIR), :]

    def forward(p, carry):
        layer(
            p,
            dot(tile_ref[p, 0], x_pair(p - 1))
            + dot(tile_ref[p, 1], x_pair(p))
            + dot(tile_ref[p, 2], x_pair(p + 1)),
        )
        return carry

    lax.fori_loop(1, PAIRS - 1, forward, 0)

    pl.semaphore_wait(entry, 2 + 3 + 15 + 3 + 1)

    def rim(side):
        return pltpu.make_async_remote_copy(
            src_ref=x_ref.at[pl.ds((1 - side) * (PAIRS - 1) * PAIR, PAIR)],
            dst_ref=halo.at[side],
            send_sem=halo_send.at[side],
            recv_sem=halo_recv.at[side],
            device_id=along(1 - 2 * side),
            device_id_type=MESH,
        )

    rim(0).start()
    rim(1).start()

    def edge_start(side, carry):
        p = side * (PAIRS - 1)
        edge_acc[side] = dot(tile_ref[p, 1], x_pair(p)) + dot(
            tile_ref[p, 2 - 2 * side], x_pair(1 + 3 * side)
        )
        return carry

    lax.fori_loop(0, 2, edge_start, 0)

    def inner(side, carry):
        near = 1 + 3 * side
        deep = 2 + side
        gf_acc[side] = dot_t(tile_ref[near, 1], u_ref[near]) + dot_t(
            tile_ref[deep, 2 * side], u_ref[deep]
        )
        gf_edge[side] = dot_t(tile_ref[near, 2 * side], u_ref[near])
        total = (
            dot_t(tile_ref[deep - 1, 2], u_ref[deep - 1])
            + dot_t(tile_ref[deep, 1], u_ref[deep])
            + dot_t(tile_ref[deep + 1, 0], u_ref[deep + 1])
        )
        gf_ref[pl.ds(pl.multiple_of(deep * PAIR, PAIR), PAIR), :] = total.astype(BF16)
        return carry

    lax.fori_loop(0, 2, inner, 0)

    def back_copy(side):
        return pltpu.make_async_remote_copy(
            src_ref=spill.at[side],
            dst_ref=landed.at[1 - side],
            send_sem=spill_send.at[side],
            recv_sem=spill_recv.at[1 - side],
            device_id=along(2 * side - 1),
            device_id_type=MESH,
        )

    def edge(side, carry):
        p = side * (PAIRS - 1)
        rim(side).wait_recv()
        layer(p, edge_acc[side] + dot(tile_ref[p, 2 * side], halo[side]))
        up = u_ref[p]
        spill[side] = dot_t(tile_ref[p, 2 * side], up).astype(BF16)
        back_copy(side).start()
        near = 1 + 3 * side
        gf_ref[pl.ds(pl.multiple_of(near * PAIR, PAIR), PAIR), :] = (
            gf_acc[side] + dot_t(tile_ref[p, 2 - 2 * side], up)
        ).astype(BF16)
        gf_edge[side] += dot_t(tile_ref[p, 1], up)
        return carry

    lax.fori_loop(0, 2, edge, 0)

    grad_half[0, pl.ds(PAIR, 8)] = bias_acc[:, :BLK]
    grad_half[1, pl.ds(PAIR, 8)] = bias_acc[:, BLK:]
    to_core = pltpu.make_async_remote_copy(
        src_ref=grad_half.at[1 - core], dst_ref=from_core, send_sem=core_send, recv_sem=core_recv,
        device_id=other_core, device_id_type=MESH,
    )
    to_core.start()
    inner_rows = pl.ds(PAIR, (PAIRS - 2) * PAIR)
    saves = [
        pltpu.make_async_copy(act_ref, act_hbm, save_sem.at[0]),
        pltpu.make_async_copy(gf_ref.at[inner_rows], gf_hbm.at[inner_rows], save_sem.at[1]),
    ]
    for save in saves:
        save.start()
    to_core.wait()
    bias_rows = grad_half[core, pl.ds(PAIR, 8)] + from_core[pl.ds(PAIR, 8)]
    for j in range(PLANE):
        rows = pl.ds(j * PIECE, PIECE)
        plane_out[j, pl.ds(0, PIECE)] = grad_half[core, rows] + from_core[rows]
        plane_out[j, pl.ds(PIECE, 8)] = bias_rows

    def plane_copy(step):
        j, target = plane_peer(step)
        return pltpu.make_async_remote_copy(
            src_ref=plane_out.at[j], dst_ref=plane_in.at[mine],
            send_sem=plane_send.at[j], recv_sem=plane_recv.at[mine],
            device_id=target, device_id_type=MESH,
        )

    def plane_arrival(step):
        j, target = plane_peer(step)
        return pltpu.make_async_remote_copy(
            src_ref=plane_out.at[j], dst_ref=plane_in.at[j],
            send_sem=plane_send.at[j], recv_sem=plane_recv.at[j],
            device_id=target, device_id_type=MESH,
        )

    for step in range(1, PLANE):
        plane_copy(step).start()
    plane_in[mine] = plane_out[mine]
    for step in range(1, PLANE):
        plane_arrival(step).wait()
    total = plane_in[0]
    for j in range(1, PLANE):
        total = total + plane_in[j]

    z_near[member] = total

    def near_copy(step):
        return pltpu.make_async_remote_copy(
            src_ref=z_near.at[member], dst_ref=z_near.at[member],
            send_sem=near_send.at[step - 1], recv_sem=near_recv.at[member],
            device_id=near_peer(step), device_id_type=MESH,
        )

    def near_arrival(step):
        m = (member + step) % 4
        return pltpu.make_async_remote_copy(
            src_ref=z_near.at[m], dst_ref=z_near.at[m],
            send_sem=near_send.at[step - 1], recv_sem=near_recv.at[m],
            device_id=near_peer(step), device_id_type=MESH,
        )

    for step in range(1, 4):
        near_copy(step).start()
    for step in range(1, 4):
        near_arrival(step).wait()
    z_far[group] = (z_near[0] + z_near[1]) + (z_near[2] + z_near[3])

    def far_copy(step):
        return pltpu.make_async_remote_copy(
            src_ref=z_far.at[group], dst_ref=z_far.at[group],
            send_sem=far_send.at[step - 1], recv_sem=far_recv.at[group],
            device_id=far_peer(step), device_id_type=MESH,
        )

    def far_arrival(step):
        g = (group + step) % 4
        return pltpu.make_async_remote_copy(
            src_ref=z_far.at[g], dst_ref=z_far.at[g],
            send_sem=far_send.at[step - 1], recv_sem=far_recv.at[g],
            device_id=far_peer(step), device_id_type=MESH,
        )

    for step in range(1, 4):
        far_copy(step).start()

    def finish(side):
        back_copy(1 - side).wait_recv()
        rows = pl.ds(side * (PAIRS - 1) * PAIR, PAIR)
        gf_ref[rows, :] = (gf_edge[side] + landed[side].astype(F32)).astype(BF16)
        save = pltpu.make_async_copy(gf_ref.at[rows], gf_hbm.at[rows], save_sem.at[2 + side])
        save.start()
        return save

    for step in range(1, 4):
        far_arrival(step).wait()
    total = ((z_far[0] + z_far[1]) + (z_far[2] + z_far[3])) * norm_scale
    full_half[pl.ds(pl.multiple_of(mine * PIECE, PIECE), PIECE), :] = total[:PIECE]
    full_half[pl.ds(PAIR, 8), :] = jnp.broadcast_to(jnp.sum(total[PIECE:], axis=0, keepdims=True), (8, BLK))

    def piece(j):
        return full_half.at[pl.ds(pl.multiple_of(j * PIECE, PIECE), PIECE)]

    def gather_copy(step):
        j, target = plane_peer(step)
        return pltpu.make_async_remote_copy(
            src_ref=piece(mine), dst_ref=piece(mine),
            send_sem=gather_send.at[j], recv_sem=gather_recv.at[mine],
            device_id=target, device_id_type=MESH,
        )

    def gather_arrival(step):
        j, target = plane_peer(step)
        return pltpu.make_async_remote_copy(
            src_ref=piece(j), dst_ref=piece(j),
            send_sem=gather_send.at[j], recv_sem=gather_recv.at[j],
            device_id=target, device_id_type=MESH,
        )

    for step in range(1, PLANE):
        gather_copy(step).start()
    saves.append(finish(1))
    for step in range(1, PLANE):
        gather_arrival(step).wait()
    across = pltpu.make_async_remote_copy(
        src_ref=full_half, dst_ref=other_half, send_sem=back_send, recv_sem=back_recv,
        device_id=other_core, device_id_type=MESH,
    )
    across.start()
    across.wait()
    low = jnp.where(core == 0, full_half[...], other_half[...])
    high = jnp.where(core == 0, other_half[...], full_half[...])
    gw_ref[:, :BLK] = low[:PAIR]
    gw_ref[:, BLK:] = high[:PAIR]
    gb_ref[:, :BLK] = low[PAIR : PAIR + 1]
    gb_ref[:, BLK:] = high[PAIR : PAIR + 1]
    saves.append(finish(0))
    for side in range(2):
        rim(side).wait_send()
        back_copy(side).wait_send()
    for save in saves:
        save.wait()


def on_device(features, adj_values, adj_offset, adj_count, weight, bias_vector, cotangent):
    import functools

    nodes, width = features.shape
    nodes_total = nodes * lax.axis_size("rows") * lax.axis_size("cols")
    vmem = pl.BlockSpec(memory_space=pltpu.VMEM)
    smem = pl.BlockSpec(memory_space=pltpu.SMEM)
    anywhere = pl.BlockSpec(memory_space=pl.ANY)
    sem = pltpu.SemaphoreType.DMA
    activated, grad_features, grad_weight, grad_bias = pl.pallas_call(
        functools.partial(kernel, 1.0 / math.sqrt(nodes_total)),
        out_shape=(
            jax.ShapeDtypeStruct((nodes, width), BF16),
            jax.ShapeDtypeStruct((nodes, width), BF16),
            jax.ShapeDtypeStruct((width, width), F32),
            jax.ShapeDtypeStruct((1, width), F32),
        ),
        in_specs=[anywhere, anywhere, smem, smem, vmem, vmem, anywhere],
        out_specs=(anywhere, anywhere, vmem, vmem),
        scratch_shapes=[
            pltpu.VMEM((nodes, width), BF16),
            pltpu.VMEM((2 * PAIRS + 1, SLOTS, BLK, BLK), BF16),
            pltpu.VMEM((nodes, width), BF16),
            pltpu.VMEM((PAIRS, 3, PAIR, PAIR), BF16),
            pltpu.VMEM((2, PAIR, width), F32),
            pltpu.VMEM((PAIRS, PAIR, width), BF16),
            pltpu.VMEM((nodes, width), BF16),
            pltpu.VMEM((nodes, width), BF16),
            pltpu.VMEM((2, PAIR, width), F32),
            pltpu.VMEM((2, PAIR, width), F32),
            pltpu.VMEM((2, PAIR, width), BF16),
            pltpu.VMEM((2, PAIR, width), BF16),
            pltpu.VMEM((2, PAIR, width), BF16),
            pltpu.VMEM((2, PAIR + 8, BLK), F32),
            pltpu.VMEM((8, width), F32),
            pltpu.VMEM((PAIR + 8, BLK), F32),
            pltpu.VMEM((PLANE, PIECE + 8, BLK), F32),
            pltpu.VMEM((PLANE, PIECE + 8, BLK), F32),
            pltpu.VMEM((4, PIECE + 8, BLK), F32),
            pltpu.VMEM((4, PIECE + 8, BLK), F32),
            pltpu.VMEM((PAIR + 8, BLK), F32),
            pltpu.VMEM((PAIR + 8, BLK), F32),
            sem((3,)), sem((4,)), sem((2,)), sem((2,)), sem((2,)), sem((2,)),
            sem, sem, sem((PLANE,)), sem((PLANE,)), sem((3,)), sem((4,)), sem((3,)), sem((4,)),
            sem((PLANE,)), sem((PLANE,)), sem, sem,
        ],
        compiler_params=pltpu.CompilerParams(
            collective_id=0, has_side_effects=True, vmem_limit_bytes=56 << 20
        ),
        name="graph_layer",
    )(features, adj_values, adj_offset, adj_count, weight, bias_vector.reshape(1, width), cotangent)
    return activated, grad_features, grad_weight, grad_bias.reshape(width)


def solution(mesh):
    both = ("rows", "cols")
    return jax.shard_map(
        on_device,
        mesh=mesh,
        in_specs=(P(both, None), P(both, None, None, None), P(both, None), P(both), P(), P(), P(both, None)),
        out_specs=(P(both, None), P(both, None), P(), P()),
        check_vma=False,
    )
```

```python
import functools
import math

import jax
import jax.numpy as jnp
from jax import lax
from jax.experimental import pallas as pl
from jax.experimental.pallas import tpu as pltpu
from jax.sharding import PartitionSpec as P

MESH = pl.DeviceIdType.MESH
F32 = jnp.float32
BF16 = jnp.bfloat16
BLK = 128
PAIR = 256
PAIRS = 6
SLOTS = 3
PLANE = 16
PARTS = 4
PIECE = 16


def dot(a, b):
    return jnp.dot(a, b, preferred_element_type=F32)


def dot_t(a, b):
    return lax.dot_general(a, b, (((0,), (0,)), ((), ())), preferred_element_type=F32)


def place():
    rows, cols = lax.axis_index("rows"), lax.axis_index("cols")
    return rows // 16, cols // 2, (cols % 2) * 8 + (rows // 2) % 8, rows % 2


def device(x, y, z, core):
    return ((x * 8 + z % 8) * 2 + core, y * 2 + z // 8)


def along(step):
    flat = (lax.axis_index("rows") * 8 + lax.axis_index("cols") + step + 512) % 512
    return (flat // 8, flat % 8)


def kernel(
    norm_scale,
    feat_hbm, adj_hbm, off_ref, cnt_ref, w_ref, bias_ref, cot_hbm,
    act_ref, gf_ref, gw_ref, gb_ref,
    x_ref, a_ref, cot_ref, tile_ref, edge_acc, u_ref, gf_acc, gf_edge,
    halo, spill, landed, grad_half, bias_acc,
    from_core, plane_out, plane_in, z_near, z_far, full_half, other_half,
    load_sem, halo_send, halo_recv, spill_send, spill_recv,
    core_send, core_recv, plane_send, plane_recv, near_send, near_recv, far_send, far_recv,
    gather_send, gather_recv, back_send, back_recv,
):
    x, y, z, core = place()
    mine = x * 4 + y
    group, member = z // 4, z % 4

    def plane_peer(step):
        j = (mine + step) % PLANE
        return j, device(j // 4, j % 4, z, core)

    def near_peer(step):
        m = (member + step) % 4
        return device(x, y, group * 4 + m, core)

    def far_peer(step):
        g = (group + step) % 4
        return device(x, y, g * 4 + member, core)

    other_core = device(x, y, z, 1 - core)

    entry = pltpu.get_barrier_semaphore()

    def greet(target):
        pl.semaphore_signal(entry, inc=1, device_id=target, device_id_type=MESH)

    greet(along(1))
    greet(along(-1))
    for step in range(1, 4):
        greet(far_peer(step))
    for step in range(1, PLANE):
        greet(plane_peer(step)[1])
    for step in range(1, 4):
        greet(near_peer(step))
    greet(other_core)

    loads = [
        pltpu.make_async_copy(adj_hbm, a_ref.at[pl.ds(0, 2 * PAIRS)], load_sem.at[0]),
        pltpu.make_async_copy(feat_hbm, x_ref, load_sem.at[1]),
        pltpu.make_async_copy(cot_hbm, cot_ref, load_sem.at[2]),
    ]
    for load in loads:
        load.start()
    for s in range(SLOTS):
        a_ref[2 * PAIRS, s] = jnp.zeros((BLK, BLK), BF16)
    bias_acc[...] = jnp.zeros_like(bias_acc)
    grad_half[...] = jnp.zeros_like(grad_half)
    loads[0].wait()

    def build(p, carry):
        for r in range(2):
            i = 2 * p + r
            count = cnt_ref[i]
            offs = [off_ref[s, i] for s in range(SLOTS)]
            for q in range(3):
                for c in range(2):
                    k = 2 * (q - 1) + c - r
                    at = (pl.ds(r * BLK, BLK), pl.ds(c * BLK, BLK))
                    if abs(k) > 2:
                        tile_ref[p, q, at[0], at[1]] = jnp.zeros((BLK, BLK), BF16)
                        continue
                    row, slot = jnp.int32(2 * PAIRS), jnp.int32(0)
                    for s in range(SLOTS):
                        hit = jnp.logical_and(offs[s] == k, s < count)
                        row = jnp.where(hit, i, row)
                        slot = jnp.where(hit, s, slot)
                    tile_ref[p, q, at[0], at[1]] = a_ref[row, slot]
        return carry

    lax.fori_loop(0, PAIRS, build, 0)
    loads[1].wait()
    loads[2].wait()

    def layer(p, summed):
        rows = pl.ds(pl.multiple_of(p * PAIR, PAIR), PAIR)
        agg = summed.astype(BF16)
        pre = dot(agg, w_ref[...]) + bias_ref[...]
        q = jax.nn.sigmoid(pre)
        act_ref[rows, :] = (pre * q).astype(BF16)
        grad_pre = (cot_ref[rows, :].astype(F32) * q * (1.0 + pre * (1.0 - q))).astype(BF16)
        up = lax.dot_general(
            grad_pre, w_ref[...], (((1,), (1,)), ((), ())), preferred_element_type=F32
        ).astype(BF16)
        u_ref[p] = up
        gw = dot_t(agg, grad_pre)
        grad_half[0, pl.ds(0, PAIR)] += gw[:, :BLK]
        grad_half[1, pl.ds(0, PAIR)] += gw[:, BLK:]
        bias_acc[...] += jnp.sum(grad_pre.astype(F32).reshape(PAIR // 8, 8, PAIR), axis=0)

    def x_pair(p):
        return x_ref[pl.ds(pl.multiple_of(p * PAIR, PAIR), PAIR), :]

    def forward(p, carry):
        layer(
            p,
            dot(tile_ref[p, 0], x_pair(p - 1))
            + dot(tile_ref[p, 1], x_pair(p))
            + dot(tile_ref[p, 2], x_pair(p + 1)),
        )
        return carry

    lax.fori_loop(1, PAIRS - 1, forward, 0)

    pl.semaphore_wait(entry, 2 + 3 + 15 + 3 + 1)

    def rim(side):
        return pltpu.make_async_remote_copy(
            src_ref=x_ref.at[pl.ds((1 - side) * (PAIRS - 1) * PAIR, PAIR)],
            dst_ref=halo.at[side],
            send_sem=halo_send.at[side],
            recv_sem=halo_recv.at[side],
            device_id=along(1 - 2 * side),
            device_id_type=MESH,
        )

    rim(0).start()

    def edge_start(side, carry):
        p = side * (PAIRS - 1)
        edge_acc[side] = dot(tile_ref[p, 1], x_pair(p)) + dot(
            tile_ref[p, 2 - 2 * side], x_pair(1 + 3 * side)
        )
        return carry

    lax.fori_loop(0, 2, edge_start, 0)

    def inner(side, carry):
        near = 1 + 3 * side
        deep = 2 + side
        gf_acc[side] = dot_t(tile_ref[near, 1], u_ref[near]) + dot_t(
            tile_ref[deep, 2 * side], u_ref[deep]
        )
        gf_edge[side] = dot_t(tile_ref[near, 2 * side], u_ref[near])
        total = (
            dot_t(tile_ref[deep - 1, 2], u_ref[deep - 1])
            + dot_t(tile_ref[deep, 1], u_ref[deep])
            + dot_t(tile_ref[deep + 1, 0], u_ref[deep + 1])
        )
        gf_ref[pl.ds(pl.multiple_of(deep * PAIR, PAIR), PAIR), :] = total.astype(BF16)
        return carry

    lax.fori_loop(0, 2, inner, 0)
    rim(0).wait_send()
    rim(1).start()

    def back_copy(side, part):
        rows = pl.ds(part * (PAIR // PARTS), PAIR // PARTS)
        return pltpu.make_async_remote_copy(
            src_ref=spill.at[side, rows],
            dst_ref=landed.at[1 - side, rows],
            send_sem=spill_send.at[side, part],
            recv_sem=spill_recv.at[1 - side, part],
            device_id=along(2 * side - 1),
            device_id_type=MESH,
        )

    def edge_layer(side):
        p = side * (PAIRS - 1)
        rim(side).wait_recv()
        layer(p, edge_acc[side] + dot(tile_ref[p, 2 * side], halo[side]))

    def edge_back(side):
        p = side * (PAIRS - 1)
        up = u_ref[p]
        spill[side] = dot_t(tile_ref[p, 2 * side], up).astype(BF16)
        if side == 0:
            for part in range(PARTS):
                back_copy(0, part).start()
        near = 1 + 3 * side
        gf_ref[pl.ds(near * PAIR, PAIR), :] = (
            gf_acc[side] + dot_t(tile_ref[p, 2 - 2 * side], up)
        ).astype(BF16)
        gf_edge[side] += dot_t(tile_ref[p, 1], up)

    edge_layer(0)
    edge_back(0)
    edge_layer(1)

    grad_half[0, pl.ds(PAIR, 8)] = bias_acc[:, :BLK]
    grad_half[1, pl.ds(PAIR, 8)] = bias_acc[:, BLK:]
    to_core = pltpu.make_async_remote_copy(
        src_ref=grad_half.at[1 - core], dst_ref=from_core, send_sem=core_send, recv_sem=core_recv,
        device_id=other_core, device_id_type=MESH,
    )
    to_core.start()
    edge_back(1)
    back_copy(1, 0).start()
    to_core.wait()
    bias_rows = grad_half[core, pl.ds(PAIR, 8)] + from_core[pl.ds(PAIR, 8)]
    for j in range(PLANE):
        rows = pl.ds(j * PIECE, PIECE)
        plane_out[j, pl.ds(0, PIECE)] = grad_half[core, rows] + from_core[rows]
        plane_out[j, pl.ds(PIECE, 8)] = bias_rows

    def plane_copy(step):
        j, target = plane_peer(step)
        return pltpu.make_async_remote_copy(
            src_ref=plane_out.at[j], dst_ref=plane_in.at[mine],
            send_sem=plane_send.at[j], recv_sem=plane_recv.at[mine],
            device_id=target, device_id_type=MESH,
        )

    def plane_arrival(step):
        j, target = plane_peer(step)
        return pltpu.make_async_remote_copy(
            src_ref=plane_out.at[j], dst_ref=plane_in.at[j],
            send_sem=plane_send.at[j], recv_sem=plane_recv.at[j],
            device_id=target, device_id_type=MESH,
        )

    for step in range(1, PLANE):
        plane_copy(step).start()
    plane_in[mine] = plane_out[mine]
    for step in range(1, PLANE):
        plane_arrival(step).wait()
    total = plane_in[0]
    for j in range(1, PLANE):
        total = total + plane_in[j]

    z_near[member] = total

    def near_copy(step):
        return pltpu.make_async_remote_copy(
            src_ref=z_near.at[member], dst_ref=z_near.at[member],
            send_sem=near_send.at[step - 1], recv_sem=near_recv.at[member],
            device_id=near_peer(step), device_id_type=MESH,
        )

    def near_arrival(step):
        m = (member + step) % 4
        return pltpu.make_async_remote_copy(
            src_ref=z_near.at[m], dst_ref=z_near.at[m],
            send_sem=near_send.at[step - 1], recv_sem=near_recv.at[m],
            device_id=near_peer(step), device_id_type=MESH,
        )

    for step in range(1, 4):
        near_copy(step).start()
    back_copy(1, 1).start()
    for step in range(1, 4):
        near_arrival(step).wait()
    z_far[group] = (z_near[0] + z_near[1]) + (z_near[2] + z_near[3])

    def far_copy(step):
        return pltpu.make_async_remote_copy(
            src_ref=z_far.at[group], dst_ref=z_far.at[group],
            send_sem=far_send.at[step - 1], recv_sem=far_recv.at[group],
            device_id=far_peer(step), device_id_type=MESH,
        )

    def far_arrival(step):
        g = (group + step) % 4
        return pltpu.make_async_remote_copy(
            src_ref=z_far.at[g], dst_ref=z_far.at[g],
            send_sem=far_send.at[step - 1], recv_sem=far_recv.at[g],
            device_id=far_peer(step), device_id_type=MESH,
        )

    for step in range(1, 4):
        far_copy(step).start()
    back_copy(1, 2).start()
    back_copy(1, 3).start()

    def finish(side):
        for part in range(PARTS):
            back_copy(1 - side, part).wait_recv()
        rows = pl.ds(side * (PAIRS - 1) * PAIR, PAIR)
        gf_ref[rows, :] = (gf_edge[side] + landed[side].astype(F32)).astype(BF16)

    for step in range(1, 4):
        far_arrival(step).wait()
    total = ((z_far[0] + z_far[1]) + (z_far[2] + z_far[3])) * norm_scale
    full_half[pl.ds(pl.multiple_of(mine * PIECE, PIECE), PIECE), :] = total[:PIECE]
    full_half[pl.ds(PAIR, 8), :] = jnp.broadcast_to(jnp.sum(total[PIECE:], axis=0, keepdims=True), (8, BLK))

    def piece(j):
        return full_half.at[pl.ds(pl.multiple_of(j * PIECE, PIECE), PIECE)]

    def gather_copy(step):
        j, target = plane_peer(step)
        return pltpu.make_async_remote_copy(
            src_ref=piece(mine), dst_ref=piece(mine),
            send_sem=gather_send.at[j], recv_sem=gather_recv.at[mine],
            device_id=target, device_id_type=MESH,
        )

    def gather_arrival(step):
        j, target = plane_peer(step)
        return pltpu.make_async_remote_copy(
            src_ref=piece(j), dst_ref=piece(j),
            send_sem=gather_send.at[j], recv_sem=gather_recv.at[j],
            device_id=target, device_id_type=MESH,
        )

    for step in range(1, PLANE):
        gather_copy(step).start()
    finish(1)
    for step in range(1, PLANE):
        gather_arrival(step).wait()
    across = pltpu.make_async_remote_copy(
        src_ref=full_half, dst_ref=other_half, send_sem=back_send, recv_sem=back_recv,
        device_id=other_core, device_id_type=MESH,
    )
    across.start()
    across.wait()
    low = jnp.where(core == 0, full_half[...], other_half[...])
    high = jnp.where(core == 0, other_half[...], full_half[...])
    gw_ref[:, :BLK] = low[:PAIR]
    gw_ref[:, BLK:] = high[:PAIR]
    gb_ref[:, :BLK] = low[PAIR : PAIR + 1]
    gb_ref[:, BLK:] = high[PAIR : PAIR + 1]
    finish(0)
    rim(1).wait_send()
    for side in range(2):
        for part in range(PARTS):
            back_copy(side, part).wait_send()


def write_out(*refs):
    sems = refs[-1]
    copies = [pltpu.make_async_copy(refs[k], refs[4 + k], sems.at[k]) for k in range(4)]
    for copy in copies:
        copy.start()
    for copy in copies:
        copy.wait()


def on_device(features, adj_values, adj_offset, adj_count, weight, bias_vector, cotangent):
    nodes, width = features.shape
    nodes_total = nodes * lax.axis_size("rows") * lax.axis_size("cols")
    vmem = pl.BlockSpec(memory_space=pltpu.VMEM)
    smem = pl.BlockSpec(memory_space=pltpu.SMEM)
    anywhere = pl.BlockSpec(memory_space=pl.ANY)
    sem = pltpu.SemaphoreType.DMA
    results = pl.pallas_call(
        functools.partial(kernel, 1.0 / math.sqrt(nodes_total)),
        out_shape=(
            pltpu.VMEM((nodes, width), BF16),
            pltpu.VMEM((nodes, width), BF16),
            pltpu.VMEM((width, width), F32),
            pltpu.VMEM((1, width), F32),
        ),
        in_specs=[anywhere, anywhere, smem, smem, vmem, vmem, anywhere],
        out_specs=(vmem, vmem, vmem, vmem),
        scratch_shapes=[
            pltpu.VMEM((nodes, width), BF16),
            pltpu.VMEM((2 * PAIRS + 1, SLOTS, BLK, BLK), BF16),
            pltpu.VMEM((nodes, width), BF16),
            pltpu.VMEM((PAIRS, 3, PAIR, PAIR), BF16),
            pltpu.VMEM((2, PAIR, width), F32),
            pltpu.VMEM((PAIRS, PAIR, width), BF16),
            pltpu.VMEM((2, PAIR, width), F32),
            pltpu.VMEM((2, PAIR, width), F32),
            pltpu.VMEM((2, PAIR, width), BF16),
            pltpu.VMEM((2, PAIR, width), BF16),
            pltpu.VMEM((2, PAIR, width), BF16),
            pltpu.VMEM((2, PAIR + 8, BLK), F32),
            pltpu.VMEM((8, width), F32),
            pltpu.VMEM((PAIR + 8, BLK), F32),
            pltpu.VMEM((PLANE, PIECE + 8, BLK), F32),
            pltpu.VMEM((PLANE, PIECE + 8, BLK), F32),
            pltpu.VMEM((4, PIECE + 8, BLK), F32),
            pltpu.VMEM((4, PIECE + 8, BLK), F32),
            pltpu.VMEM((PAIR + 8, BLK), F32),
            pltpu.VMEM((PAIR + 8, BLK), F32),
            sem((3,)), sem((2,)), sem((2,)), sem((2, PARTS)), sem((2, PARTS)),
            sem, sem, sem((PLANE,)), sem((PLANE,)), sem((3,)), sem((4,)), sem((3,)), sem((4,)),
            sem((PLANE,)), sem((PLANE,)), sem, sem,
        ],
        compiler_params=pltpu.CompilerParams(
            collective_id=0, has_side_effects=True, vmem_limit_bytes=56 << 20
        ),
        name="graph_layer",
    )(features, adj_values, adj_offset.T, adj_count, weight, bias_vector.reshape(1, width), cotangent)
    activated, grad_features, grad_weight, grad_bias = pl.pallas_call(
        write_out,
        out_shape=(
            jax.ShapeDtypeStruct((nodes, width), BF16),
            jax.ShapeDtypeStruct((nodes, width), BF16),
            jax.ShapeDtypeStruct((width, width), F32),
            jax.ShapeDtypeStruct((1, width), F32),
        ),
        in_specs=[vmem] * 4,
        out_specs=(anywhere,) * 4,
        scratch_shapes=[sem((4,))],
        name="write_out",
    )(*[pltpu.with_memory_space_constraint(r, pltpu.VMEM) for r in results])
    return activated, grad_features, grad_weight, grad_bias.reshape(width)


def solution(mesh):
    both = ("rows", "cols")
    return jax.shard_map(
        on_device,
        mesh=mesh,
        in_specs=(P(both, None), P(both, None, None, None), P(both, None), P(both), P(), P(), P(both, None)),
        out_specs=(P(both, None), P(both, None), P(), P()),
        check_vma=False,
    )
```

```python
import functools
import math

import jax
import jax.numpy as jnp
from jax import lax
from jax.experimental import pallas as pl
from jax.experimental.pallas import tpu as pltpu
from jax.sharding import PartitionSpec as P

MESH = pl.DeviceIdType.MESH
F32 = jnp.float32
BF16 = jnp.bfloat16
BLK = 128
PAIR = 256
PAIRS = 6
SLOTS = 3
PLANE = 16
PARTS = 4
PIECE = 16


def dot(a, b):
    return jnp.dot(a, b, preferred_element_type=F32)


def dot_t(a, b):
    return lax.dot_general(a, b, (((0,), (0,)), ((), ())), preferred_element_type=F32)


def place():
    rows, cols = lax.axis_index("rows"), lax.axis_index("cols")
    return rows // 16, cols // 2, (cols % 2) * 8 + (rows // 2) % 8, rows % 2


def device(x, y, z, core):
    return ((x * 8 + z % 8) * 2 + core, y * 2 + z // 8)


def along(step):
    flat = (lax.axis_index("rows") * 8 + lax.axis_index("cols") + step + 512) % 512
    return (flat // 8, flat % 8)


def kernel(
    norm_scale,
    feat_hbm, adj_hbm, off_ref, cnt_ref, w_ref, bias_ref, cot_hbm,
    act_ref, gf_ref, gw_ref, gb_ref,
    x_ref, a_ref, cot_ref, tile_ref, edge_acc, u_ref, gf_acc, gf_edge,
    halo, spill, landed, grad_half, bias_acc,
    from_core, plane_out, plane_in, z_near, z_far, full_half, other_half,
    load_sem, halo_send, halo_recv, spill_send, spill_recv,
    core_send, core_recv, plane_send, plane_recv, near_send, near_recv, far_send, far_recv,
    gather_send, gather_recv, back_send, back_recv,
):
    x, y, z, core = place()
    mine = x * 4 + y
    group, member = z // 4, z % 4

    def plane_peer(step):
        j = (mine + step) % PLANE
        return j, device(j // 4, j % 4, z, core)

    def near_peer(step):
        m = (member + step) % 4
        return device(x, y, group * 4 + m, core)

    def far_peer(step):
        g = (group + step) % 4
        return device(x, y, g * 4 + member, core)

    other_core = device(x, y, z, 1 - core)

    entry = pltpu.get_barrier_semaphore()

    def greet(target):
        pl.semaphore_signal(entry, inc=1, device_id=target, device_id_type=MESH)

    greet(along(1))
    greet(along(-1))
    for step in range(1, 4):
        greet(far_peer(step))
    for step in range(1, PLANE):
        greet(plane_peer(step)[1])
    for step in range(1, 4):
        greet(near_peer(step))
    greet(other_core)

    loads = [
        pltpu.make_async_copy(adj_hbm, a_ref.at[pl.ds(0, 2 * PAIRS)], load_sem.at[0]),
        pltpu.make_async_copy(feat_hbm, x_ref, load_sem.at[1]),
        pltpu.make_async_copy(cot_hbm, cot_ref, load_sem.at[2]),
    ]
    for load in loads:
        load.start()
    for s in range(SLOTS):
        a_ref[2 * PAIRS, s] = jnp.zeros((BLK, BLK), BF16)
    bias_acc[...] = jnp.zeros_like(bias_acc)
    grad_half[...] = jnp.zeros_like(grad_half)
    loads[0].wait()

    def build(p, carry):
        for r in range(2):
            i = 2 * p + r
            count = cnt_ref[i]
            offs = [off_ref[s, i] for s in range(SLOTS)]
            for q in range(3):
                for c in range(2):
                    k = 2 * (q - 1) + c - r
                    at = (pl.ds(r * BLK, BLK), pl.ds(c * BLK, BLK))
                    if abs(k) > 2:
                        tile_ref[p, q, at[0], at[1]] = jnp.zeros((BLK, BLK), BF16)
                        continue
                    row, slot = jnp.int32(2 * PAIRS), jnp.int32(0)
                    for s in range(SLOTS):
                        hit = jnp.logical_and(offs[s] == k, s < count)
                        row = jnp.where(hit, i, row)
                        slot = jnp.where(hit, s, slot)
                    tile_ref[p, q, at[0], at[1]] = a_ref[row, slot]
        return carry

    lax.fori_loop(0, PAIRS, build, 0)
    loads[1].wait()
    loads[2].wait()

    def layer(p, summed):
        rows = pl.ds(pl.multiple_of(p * PAIR, PAIR), PAIR)
        agg = summed.astype(BF16)
        pre = dot(agg, w_ref[...]) + bias_ref[...]
        q = jax.nn.sigmoid(pre)
        act_ref[rows, :] = (pre * q).astype(BF16)
        grad_pre = (cot_ref[rows, :].astype(F32) * q * (1.0 + pre * (1.0 - q))).astype(BF16)
        up = lax.dot_general(
            grad_pre, w_ref[...], (((1,), (1,)), ((), ())), preferred_element_type=F32
        ).astype(BF16)
        u_ref[p] = up
        gw = dot_t(agg, grad_pre)
        grad_half[0, pl.ds(0, PAIR)] += gw[:, :BLK]
        grad_half[1, pl.ds(0, PAIR)] += gw[:, BLK:]
        bias_acc[...] += jnp.sum(grad_pre.astype(F32).reshape(PAIR // 8, 8, PAIR), axis=0)

    def x_pair(p):
        return x_ref[pl.ds(pl.multiple_of(p * PAIR, PAIR), PAIR), :]

    def forward(p, carry):
        layer(
            p,
            dot(tile_ref[p, 0], x_pair(p - 1))
            + dot(tile_ref[p, 1], x_pair(p))
            + dot(tile_ref[p, 2], x_pair(p + 1)),
        )
        return carry

    lax.fori_loop(1, PAIRS - 1, forward, 0)

    pl.semaphore_wait(entry, 2 + 3 + 15 + 3 + 1)

    def rim(side):
        return pltpu.make_async_remote_copy(
            src_ref=x_ref.at[pl.ds((1 - side) * (PAIRS - 1) * PAIR, PAIR)],
            dst_ref=halo.at[side],
            send_sem=halo_send.at[side],
            recv_sem=halo_recv.at[side],
            device_id=along(1 - 2 * side),
            device_id_type=MESH,
        )

    rim(0).start()
    rim(1).start()

    def edge_start(side, carry):
        p = side * (PAIRS - 1)
        edge_acc[side] = dot(tile_ref[p, 1], x_pair(p)) + dot(
            tile_ref[p, 2 - 2 * side], x_pair(1 + 3 * side)
        )
        return carry

    lax.fori_loop(0, 2, edge_start, 0)

    def inner(side, carry):
        near = 1 + 3 * side
        deep = 2 + side
        gf_acc[side] = dot_t(tile_ref[near, 1], u_ref[near]) + dot_t(
            tile_ref[deep, 2 * side], u_ref[deep]
        )
        gf_edge[side] = dot_t(tile_ref[near, 2 * side], u_ref[near])
        total = (
            dot_t(tile_ref[deep - 1, 2], u_ref[deep - 1])
            + dot_t(tile_ref[deep, 1], u_ref[deep])
            + dot_t(tile_ref[deep + 1, 0], u_ref[deep + 1])
        )
        gf_ref[pl.ds(pl.multiple_of(deep * PAIR, PAIR), PAIR), :] = total.astype(BF16)
        return carry

    lax.fori_loop(0, 2, inner, 0)

    def back_copy(side, part):
        rows = pl.ds(part * (PAIR // PARTS), PAIR // PARTS)
        return pltpu.make_async_remote_copy(
            src_ref=spill.at[side, rows],
            dst_ref=landed.at[1 - side, rows],
            send_sem=spill_send.at[side, part],
            recv_sem=spill_recv.at[1 - side, part],
            device_id=along(2 * side - 1),
            device_id_type=MESH,
        )

    def edge_layer(side):
        p = side * (PAIRS - 1)
        rim(side).wait_recv()
        layer(p, edge_acc[side] + dot(tile_ref[p, 2 * side], halo[side]))

    def edge_back(side):
        p = side * (PAIRS - 1)
        up = u_ref[p]
        spill[side] = dot_t(tile_ref[p, 2 * side], up).astype(BF16)
        near = 1 + 3 * side
        gf_ref[pl.ds(near * PAIR, PAIR), :] = (
            gf_acc[side] + dot_t(tile_ref[p, 2 - 2 * side], up)
        ).astype(BF16)
        gf_edge[side] += dot_t(tile_ref[p, 1], up)

    edge_layer(0)
    edge_back(0)
    edge_layer(1)

    grad_half[0, pl.ds(PAIR, 8)] = bias_acc[:, :BLK]
    grad_half[1, pl.ds(PAIR, 8)] = bias_acc[:, BLK:]
    to_core = pltpu.make_async_remote_copy(
        src_ref=grad_half.at[1 - core], dst_ref=from_core, send_sem=core_send, recv_sem=core_recv,
        device_id=other_core, device_id_type=MESH,
    )
    to_core.start()
    edge_back(1)
    back_copy(0, 0).start()
    back_copy(1, 0).start()
    to_core.wait()
    bias_rows = grad_half[core, pl.ds(PAIR, 8)] + from_core[pl.ds(PAIR, 8)]
    for j in range(PLANE):
        rows = pl.ds(j * PIECE, PIECE)
        plane_out[j, pl.ds(0, PIECE)] = grad_half[core, rows] + from_core[rows]
        plane_out[j, pl.ds(PIECE, 8)] = bias_rows

    def plane_copy(step):
        j, target = plane_peer(step)
        return pltpu.make_async_remote_copy(
            src_ref=plane_out.at[j], dst_ref=plane_in.at[mine],
            send_sem=plane_send.at[j], recv_sem=plane_recv.at[mine],
            device_id=target, device_id_type=MESH,
        )

    def plane_arrival(step):
        j, target = plane_peer(step)
        return pltpu.make_async_remote_copy(
            src_ref=plane_out.at[j], dst_ref=plane_in.at[j],
            send_sem=plane_send.at[j], recv_sem=plane_recv.at[j],
            device_id=target, device_id_type=MESH,
        )

    for step in range(1, PLANE):
        plane_copy(step).start()
    plane_in[mine] = plane_out[mine]
    for step in range(1, PLANE):
        plane_arrival(step).wait()
    total = plane_in[0]
    for j in range(1, PLANE):
        total = total + plane_in[j]

    z_near[member] = total

    def near_copy(step):
        return pltpu.make_async_remote_copy(
            src_ref=z_near.at[member], dst_ref=z_near.at[member],
            send_sem=near_send.at[step - 1], recv_sem=near_recv.at[member],
            device_id=near_peer(step), device_id_type=MESH,
        )

    def near_arrival(step):
        m = (member + step) % 4
        return pltpu.make_async_remote_copy(
            src_ref=z_near.at[m], dst_ref=z_near.at[m],
            send_sem=near_send.at[step - 1], recv_sem=near_recv.at[m],
            device_id=near_peer(step), device_id_type=MESH,
        )

    for step in range(1, 4):
        near_copy(step).start()
    back_copy(0, 1).start()
    back_copy(1, 1).start()
    for step in range(1, 4):
        near_arrival(step).wait()
    z_far[group] = (z_near[0] + z_near[1]) + (z_near[2] + z_near[3])

    def far_copy(step):
        return pltpu.make_async_remote_copy(
            src_ref=z_far.at[group], dst_ref=z_far.at[group],
            send_sem=far_send.at[step - 1], recv_sem=far_recv.at[group],
            device_id=far_peer(step), device_id_type=MESH,
        )

    def far_arrival(step):
        g = (group + step) % 4
        return pltpu.make_async_remote_copy(
            src_ref=z_far.at[g], dst_ref=z_far.at[g],
            send_sem=far_send.at[step - 1], recv_sem=far_recv.at[g],
            device_id=far_peer(step), device_id_type=MESH,
        )

    for step in range(1, 4):
        far_copy(step).start()
    back_copy(0, 2).start()
    back_copy(0, 3).start()
    back_copy(1, 2).start()
    back_copy(1, 3).start()

    def finish(side):
        for part in range(PARTS):
            back_copy(1 - side, part).wait_recv()
        rows = pl.ds(side * (PAIRS - 1) * PAIR, PAIR)
        gf_ref[rows, :] = (gf_edge[side] + landed[side].astype(F32)).astype(BF16)

    for step in range(1, 4):
        far_arrival(step).wait()
    total = ((z_far[0] + z_far[1]) + (z_far[2] + z_far[3])) * norm_scale
    full_half[pl.ds(pl.multiple_of(mine * PIECE, PIECE), PIECE), :] = total[:PIECE]
    full_half[pl.ds(PAIR, 8), :] = jnp.broadcast_to(jnp.sum(total[PIECE:], axis=0, keepdims=True), (8, BLK))

    def piece(j):
        return full_half.at[pl.ds(pl.multiple_of(j * PIECE, PIECE), PIECE)]

    def gather_copy(step):
        j, target = plane_peer(step)
        return pltpu.make_async_remote_copy(
            src_ref=piece(mine), dst_ref=piece(mine),
            send_sem=gather_send.at[j], recv_sem=gather_recv.at[mine],
            device_id=target, device_id_type=MESH,
        )

    def gather_arrival(step):
        j, target = plane_peer(step)
        return pltpu.make_async_remote_copy(
            src_ref=piece(j), dst_ref=piece(j),
            send_sem=gather_send.at[j], recv_sem=gather_recv.at[j],
            device_id=target, device_id_type=MESH,
        )

    for step in range(1, PLANE):
        gather_copy(step).start()
    finish(1)
    for step in range(1, PLANE):
        gather_arrival(step).wait()
    across = pltpu.make_async_remote_copy(
        src_ref=full_half, dst_ref=other_half, send_sem=back_send, recv_sem=back_recv,
        device_id=other_core, device_id_type=MESH,
    )
    across.start()
    across.wait()
    low = jnp.where(core == 0, full_half[...], other_half[...])
    high = jnp.where(core == 0, other_half[...], full_half[...])
    gw_ref[:, :BLK] = low[:PAIR]
    gw_ref[:, BLK:] = high[:PAIR]
    gb_ref[:, :BLK] = low[PAIR : PAIR + 1]
    gb_ref[:, BLK:] = high[PAIR : PAIR + 1]
    finish(0)
    rim(0).wait_send()
    rim(1).wait_send()
    for side in range(2):
        for part in range(PARTS):
            back_copy(side, part).wait_send()


def write_out(*refs):
    sems = refs[-1]
    copies = [pltpu.make_async_copy(refs[k], refs[4 + k], sems.at[k]) for k in range(4)]
    for copy in copies:
        copy.start()
    for copy in copies:
        copy.wait()


def on_device(features, adj_values, adj_offset, adj_count, weight, bias_vector, cotangent):
    nodes, width = features.shape
    nodes_total = nodes * lax.axis_size("rows") * lax.axis_size("cols")
    vmem = pl.BlockSpec(memory_space=pltpu.VMEM)
    smem = pl.BlockSpec(memory_space=pltpu.SMEM)
    anywhere = pl.BlockSpec(memory_space=pl.ANY)
    sem = pltpu.SemaphoreType.DMA
    results = pl.pallas_call(
        functools.partial(kernel, 1.0 / math.sqrt(nodes_total)),
        out_shape=(
            pltpu.VMEM((nodes, width), BF16),
            pltpu.VMEM((nodes, width), BF16),
            pltpu.VMEM((width, width), F32),
            pltpu.VMEM((1, width), F32),
        ),
        in_specs=[anywhere, anywhere, smem, smem, vmem, vmem, anywhere],
        out_specs=(vmem, vmem, vmem, vmem),
        scratch_shapes=[
            pltpu.VMEM((nodes, width), BF16),
            pltpu.VMEM((2 * PAIRS + 1, SLOTS, BLK, BLK), BF16),
            pltpu.VMEM((nodes, width), BF16),
            pltpu.VMEM((PAIRS, 3, PAIR, PAIR), BF16),
            pltpu.VMEM((2, PAIR, width), F32),
            pltpu.VMEM((PAIRS, PAIR, width), BF16),
            pltpu.VMEM((2, PAIR, width), F32),
            pltpu.VMEM((2, PAIR, width), F32),
            pltpu.VMEM((2, PAIR, width), BF16),
            pltpu.VMEM((2, PAIR, width), BF16),
            pltpu.VMEM((2, PAIR, width), BF16),
            pltpu.VMEM((2, PAIR + 8, BLK), F32),
            pltpu.VMEM((8, width), F32),
            pltpu.VMEM((PAIR + 8, BLK), F32),
            pltpu.VMEM((PLANE, PIECE + 8, BLK), F32),
            pltpu.VMEM((PLANE, PIECE + 8, BLK), F32),
            pltpu.VMEM((4, PIECE + 8, BLK), F32),
            pltpu.VMEM((4, PIECE + 8, BLK), F32),
            pltpu.VMEM((PAIR + 8, BLK), F32),
            pltpu.VMEM((PAIR + 8, BLK), F32),
            sem((3,)), sem((2,)), sem((2,)), sem((2, PARTS)), sem((2, PARTS)),
            sem, sem, sem((PLANE,)), sem((PLANE,)), sem((3,)), sem((4,)), sem((3,)), sem((4,)),
            sem((PLANE,)), sem((PLANE,)), sem, sem,
        ],
        compiler_params=pltpu.CompilerParams(
            collective_id=0, has_side_effects=True, vmem_limit_bytes=56 << 20
        ),
        name="graph_layer",
    )(features, adj_values, adj_offset.T, adj_count, weight, bias_vector.reshape(1, width), cotangent)
    activated, grad_features, grad_weight, grad_bias = pl.pallas_call(
        write_out,
        out_shape=(
            jax.ShapeDtypeStruct((nodes, width), BF16),
            jax.ShapeDtypeStruct((nodes, width), BF16),
            jax.ShapeDtypeStruct((width, width), F32),
            jax.ShapeDtypeStruct((1, width), F32),
        ),
        in_specs=[vmem] * 4,
        out_specs=(anywhere,) * 4,
        scratch_shapes=[sem((4,))],
        name="write_out",
    )(*[pltpu.with_memory_space_constraint(r, pltpu.VMEM) for r in results])
    return activated, grad_features, grad_weight, grad_bias.reshape(width)


def solution(mesh):
    both = ("rows", "cols")
    return jax.shard_map(
        on_device,
        mesh=mesh,
        in_specs=(P(both, None), P(both, None, None, None), P(both, None), P(both), P(), P(), P(both, None)),
        out_specs=(P(both, None), P(both, None), P(), P()),
        check_vma=False,
    )
```

```python
import functools
import math

import jax
import jax.numpy as jnp
from jax import lax
from jax.experimental import pallas as pl
from jax.experimental.pallas import tpu as pltpu
from jax.sharding import PartitionSpec as P

MESH = pl.DeviceIdType.MESH
F32 = jnp.float32
BF16 = jnp.bfloat16
BLK = 128
PAIR = 256
PAIRS = 6
SLOTS = 3
PLANE = 16
PARTS = 4
PIECE = 16


def dot(a, b):
    return jnp.dot(a, b, preferred_element_type=F32)


def dot_t(a, b):
    return lax.dot_general(a, b, (((0,), (0,)), ((), ())), preferred_element_type=F32)


def place():
    rows, cols = lax.axis_index("rows"), lax.axis_index("cols")
    return rows // 16, cols // 2, (cols % 2) * 8 + (rows // 2) % 8, rows % 2


def device(x, y, z, core):
    return ((x * 8 + z % 8) * 2 + core, y * 2 + z // 8)


def along(step):
    flat = (lax.axis_index("rows") * 8 + lax.axis_index("cols") + step + 512) % 512
    return (flat // 8, flat % 8)


def kernel(
    norm_scale,
    feat_hbm, adj_hbm, off_ref, cnt_ref, w_ref, bias_ref, cot_hbm,
    act_ref, gf_ref, gw_ref, gb_ref,
    x_ref, a_ref, cot_ref, tile_ref, edge_acc, u_ref, gf_acc, gf_edge,
    halo, spill, landed, grad_half, bias_acc,
    from_core, plane_out, plane_in, z_near, z_far, full_half, other_half,
    load_sem, halo_send, halo_recv, spill_send, spill_recv,
    core_send, core_recv, plane_send, plane_recv, near_send, near_recv, far_send, far_recv,
    gather_send, gather_recv, back_send, back_recv,
):
    x, y, z, core = place()
    mine = x * 4 + y
    group, member = z // 4, z % 4

    def plane_peer(step):
        j = (mine + step) % PLANE
        return j, device(j // 4, j % 4, z, core)

    def near_peer(step):
        m = (member + step) % 4
        return device(x, y, group * 4 + m, core)

    def far_peer(step):
        g = (group + step) % 4
        return device(x, y, g * 4 + member, core)

    other_core = device(x, y, z, 1 - core)

    entry = pltpu.get_barrier_semaphore()

    def greet(target):
        pl.semaphore_signal(entry, inc=1, device_id=target, device_id_type=MESH)

    greet(along(1))
    greet(along(-1))
    for step in range(1, 4):
        greet(far_peer(step))
    for step in range(1, PLANE):
        greet(plane_peer(step)[1])
    for step in range(1, 4):
        greet(near_peer(step))
    greet(other_core)

    loads = [
        pltpu.make_async_copy(adj_hbm, a_ref.at[pl.ds(0, 2 * PAIRS)], load_sem.at[0]),
        pltpu.make_async_copy(feat_hbm, x_ref, load_sem.at[1]),
        pltpu.make_async_copy(cot_hbm, cot_ref, load_sem.at[2]),
    ]
    for load in loads:
        load.start()
    for s in range(SLOTS):
        a_ref[2 * PAIRS, s] = jnp.zeros((BLK, BLK), BF16)
    bias_acc[...] = jnp.zeros_like(bias_acc)
    grad_half[...] = jnp.zeros_like(grad_half)
    loads[0].wait()

    def build(p, carry):
        for r in range(2):
            i = 2 * p + r
            count = cnt_ref[i]
            offs = [off_ref[s, i] for s in range(SLOTS)]
            for q in range(3):
                for c in range(2):
                    k = 2 * (q - 1) + c - r
                    at = (pl.ds(r * BLK, BLK), pl.ds(c * BLK, BLK))
                    if abs(k) > 2:
                        tile_ref[p, q, at[0], at[1]] = jnp.zeros((BLK, BLK), BF16)
                        continue
                    row, slot = jnp.int32(2 * PAIRS), jnp.int32(0)
                    for s in range(SLOTS):
                        hit = jnp.logical_and(offs[s] == k, s < count)
                        row = jnp.where(hit, i, row)
                        slot = jnp.where(hit, s, slot)
                    tile_ref[p, q, at[0], at[1]] = a_ref[row, slot]
        return carry

    lax.fori_loop(0, PAIRS, build, 0)
    loads[1].wait()
    loads[2].wait()

    def layer(p, summed):
        rows = pl.ds(pl.multiple_of(p * PAIR, PAIR), PAIR)
        agg = summed.astype(BF16)
        pre = dot(agg, w_ref[...]) + bias_ref[...]
        q = jax.nn.sigmoid(pre)
        act_ref[rows, :] = (pre * q).astype(BF16)
        grad_pre = (cot_ref[rows, :].astype(F32) * q * (1.0 + pre * (1.0 - q))).astype(BF16)
        up = lax.dot_general(
            grad_pre, w_ref[...], (((1,), (1,)), ((), ())), preferred_element_type=F32
        ).astype(BF16)
        u_ref[p] = up
        gw = dot_t(agg, grad_pre)
        grad_half[0, pl.ds(0, PAIR)] += gw[:, :BLK]
        grad_half[1, pl.ds(0, PAIR)] += gw[:, BLK:]
        bias_acc[...] += jnp.sum(grad_pre.astype(F32).reshape(PAIR // 8, 8, PAIR), axis=0)

    def x_pair(p):
        return x_ref[pl.ds(pl.multiple_of(p * PAIR, PAIR), PAIR), :]

    def forward(p, carry):
        layer(
            p,
            dot(tile_ref[p, 0], x_pair(p - 1))
            + dot(tile_ref[p, 1], x_pair(p))
            + dot(tile_ref[p, 2], x_pair(p + 1)),
        )
        return carry

    lax.fori_loop(1, PAIRS - 1, forward, 0)

    pl.semaphore_wait(entry, 2 + 3 + 15 + 3 + 1)

    def rim(side):
        return pltpu.make_async_remote_copy(
            src_ref=x_ref.at[pl.ds((1 - side) * (PAIRS - 1) * PAIR, PAIR)],
            dst_ref=halo.at[side],
            send_sem=halo_send.at[side],
            recv_sem=halo_recv.at[side],
            device_id=along(1 - 2 * side),
            device_id_type=MESH,
        )

    rim(0).start()
    rim(1).start()

    def edge_start(side, carry):
        p = side * (PAIRS - 1)
        edge_acc[side] = dot(tile_ref[p, 1], x_pair(p)) + dot(
            tile_ref[p, 2 - 2 * side], x_pair(1 + 3 * side)
        )
        return carry

    lax.fori_loop(0, 2, edge_start, 0)

    def inner(side, carry):
        near = 1 + 3 * side
        deep = 2 + side
        gf_acc[side] = dot_t(tile_ref[near, 1], u_ref[near]) + dot_t(
            tile_ref[deep, 2 * side], u_ref[deep]
        )
        gf_edge[side] = dot_t(tile_ref[near, 2 * side], u_ref[near])
        total = (
            dot_t(tile_ref[deep - 1, 2], u_ref[deep - 1])
            + dot_t(tile_ref[deep, 1], u_ref[deep])
            + dot_t(tile_ref[deep + 1, 0], u_ref[deep + 1])
        )
        gf_ref[pl.ds(pl.multiple_of(deep * PAIR, PAIR), PAIR), :] = total.astype(BF16)
        return carry

    lax.fori_loop(0, 2, inner, 0)

    def back_copy(side, part):
        rows = pl.ds(part * (PAIR // PARTS), PAIR // PARTS)
        return pltpu.make_async_remote_copy(
            src_ref=spill.at[side, rows],
            dst_ref=landed.at[1 - side, rows],
            send_sem=spill_send.at[side, part],
            recv_sem=spill_recv.at[1 - side, part],
            device_id=along(2 * side - 1),
            device_id_type=MESH,
        )

    def edge_layer(side):
        p = side * (PAIRS - 1)
        rim(side).wait_recv()
        layer(p, edge_acc[side] + dot(tile_ref[p, 2 * side], halo[side]))

    def edge_back(side):
        p = side * (PAIRS - 1)
        up = u_ref[p]
        spill[side] = dot_t(tile_ref[p, 2 * side], up).astype(BF16)
        near = 1 + 3 * side
        gf_ref[pl.ds(near * PAIR, PAIR), :] = (
            gf_acc[side] + dot_t(tile_ref[p, 2 - 2 * side], up)
        ).astype(BF16)
        gf_edge[side] += dot_t(tile_ref[p, 1], up)

    edge_layer(0)
    edge_layer(1)

    grad_half[0, pl.ds(PAIR, 8)] = bias_acc[:, :BLK]
    grad_half[1, pl.ds(PAIR, 8)] = bias_acc[:, BLK:]
    to_core = pltpu.make_async_remote_copy(
        src_ref=grad_half.at[1 - core], dst_ref=from_core, send_sem=core_send, recv_sem=core_recv,
        device_id=other_core, device_id_type=MESH,
    )
    to_core.start()
    edge_back(0)
    edge_back(1)
    back_copy(1, 0).start()
    back_copy(0, 0).start()
    to_core.wait()
    bias_rows = grad_half[core, pl.ds(PAIR, 8)] + from_core[pl.ds(PAIR, 8)]
    for j in range(PLANE):
        rows = pl.ds(j * PIECE, PIECE)
        plane_out[j, pl.ds(0, PIECE)] = grad_half[core, rows] + from_core[rows]
        plane_out[j, pl.ds(PIECE, 8)] = bias_rows

    def plane_copy(step):
        j, target = plane_peer(step)
        return pltpu.make_async_remote_copy(
            src_ref=plane_out.at[j], dst_ref=plane_in.at[mine],
            send_sem=plane_send.at[j], recv_sem=plane_recv.at[mine],
            device_id=target, device_id_type=MESH,
        )

    def plane_arrival(step):
        j, target = plane_peer(step)
        return pltpu.make_async_remote_copy(
            src_ref=plane_out.at[j], dst_ref=plane_in.at[j],
            send_sem=plane_send.at[j], recv_sem=plane_recv.at[j],
            device_id=target, device_id_type=MESH,
        )

    for step in range(1, PLANE):
        plane_copy(step).start()
    plane_in[mine] = plane_out[mine]
    for step in range(1, PLANE):
        plane_arrival(step).wait()
    total = plane_in[0]
    for j in range(1, PLANE):
        total = total + plane_in[j]

    z_near[member] = total

    def near_copy(step):
        return pltpu.make_async_remote_copy(
            src_ref=z_near.at[member], dst_ref=z_near.at[member],
            send_sem=near_send.at[step - 1], recv_sem=near_recv.at[member],
            device_id=near_peer(step), device_id_type=MESH,
        )

    def near_arrival(step):
        m = (member + step) % 4
        return pltpu.make_async_remote_copy(
            src_ref=z_near.at[m], dst_ref=z_near.at[m],
            send_sem=near_send.at[step - 1], recv_sem=near_recv.at[m],
            device_id=near_peer(step), device_id_type=MESH,
        )

    for step in range(1, 4):
        near_copy(step).start()
    back_copy(1, 1).start()
    back_copy(0, 1).start()
    for step in range(1, 4):
        near_arrival(step).wait()
    z_far[group] = (z_near[0] + z_near[1]) + (z_near[2] + z_near[3])

    def far_copy(step):
        return pltpu.make_async_remote_copy(
            src_ref=z_far.at[group], dst_ref=z_far.at[group],
            send_sem=far_send.at[step - 1], recv_sem=far_recv.at[group],
            device_id=far_peer(step), device_id_type=MESH,
        )

    def far_arrival(step):
        g = (group + step) % 4
        return pltpu.make_async_remote_copy(
            src_ref=z_far.at[g], dst_ref=z_far.at[g],
            send_sem=far_send.at[step - 1], recv_sem=far_recv.at[g],
            device_id=far_peer(step), device_id_type=MESH,
        )

    for step in range(1, 4):
        far_copy(step).start()
    back_copy(1, 2).start()
    back_copy(0, 2).start()
    back_copy(1, 3).start()
    back_copy(0, 3).start()

    def finish(side):
        for part in range(PARTS):
            back_copy(1 - side, part).wait_recv()
        rows = pl.ds(side * (PAIRS - 1) * PAIR, PAIR)
        gf_ref[rows, :] = (gf_edge[side] + landed[side].astype(F32)).astype(BF16)

    for step in range(1, 4):
        far_arrival(step).wait()
    total = ((z_far[0] + z_far[1]) + (z_far[2] + z_far[3])) * norm_scale
    full_half[pl.ds(pl.multiple_of(mine * PIECE, PIECE), PIECE), :] = total[:PIECE]
    full_half[pl.ds(PAIR, 8), :] = jnp.broadcast_to(jnp.sum(total[PIECE:], axis=0, keepdims=True), (8, BLK))

    def piece(j):
        return full_half.at[pl.ds(pl.multiple_of(j * PIECE, PIECE), PIECE)]

    def gather_copy(step):
        j, target = plane_peer(step)
        return pltpu.make_async_remote_copy(
            src_ref=piece(mine), dst_ref=piece(mine),
            send_sem=gather_send.at[j], recv_sem=gather_recv.at[mine],
            device_id=target, device_id_type=MESH,
        )

    def gather_arrival(step):
        j, target = plane_peer(step)
        return pltpu.make_async_remote_copy(
            src_ref=piece(j), dst_ref=piece(j),
            send_sem=gather_send.at[j], recv_sem=gather_recv.at[j],
            device_id=target, device_id_type=MESH,
        )

    for step in range(1, PLANE):
        gather_copy(step).start()
    for step in range(1, PLANE):
        gather_arrival(step).wait()
    across = pltpu.make_async_remote_copy(
        src_ref=full_half, dst_ref=other_half, send_sem=back_send, recv_sem=back_recv,
        device_id=other_core, device_id_type=MESH,
    )
    across.start()
    across.wait()
    low = jnp.where(core == 0, full_half[...], other_half[...])
    high = jnp.where(core == 0, other_half[...], full_half[...])
    gw_ref[:, :BLK] = low[:PAIR]
    gw_ref[:, BLK:] = high[:PAIR]
    gb_ref[:, :BLK] = low[PAIR : PAIR + 1]
    gb_ref[:, BLK:] = high[PAIR : PAIR + 1]
    finish(1)
    finish(0)
    rim(0).wait_send()
    rim(1).wait_send()
    for side in range(2):
        for part in range(PARTS):
            back_copy(side, part).wait_send()


def write_out(*refs):
    sems = refs[-1]
    copies = [pltpu.make_async_copy(refs[k], refs[4 + k], sems.at[k]) for k in range(4)]
    for copy in copies:
        copy.start()
    for copy in copies:
        copy.wait()


def on_device(features, adj_values, adj_offset, adj_count, weight, bias_vector, cotangent):
    nodes, width = features.shape
    nodes_total = nodes * lax.axis_size("rows") * lax.axis_size("cols")
    vmem = pl.BlockSpec(memory_space=pltpu.VMEM)
    smem = pl.BlockSpec(memory_space=pltpu.SMEM)
    anywhere = pl.BlockSpec(memory_space=pl.ANY)
    sem = pltpu.SemaphoreType.DMA
    results = pl.pallas_call(
        functools.partial(kernel, 1.0 / math.sqrt(nodes_total)),
        out_shape=(
            pltpu.VMEM((nodes, width), BF16),
            pltpu.VMEM((nodes, width), BF16),
            pltpu.VMEM((width, width), F32),
            pltpu.VMEM((1, width), F32),
        ),
        in_specs=[anywhere, anywhere, smem, smem, vmem, vmem, anywhere],
        out_specs=(vmem, vmem, vmem, vmem),
        scratch_shapes=[
            pltpu.VMEM((nodes, width), BF16),
            pltpu.VMEM((2 * PAIRS + 1, SLOTS, BLK, BLK), BF16),
            pltpu.VMEM((nodes, width), BF16),
            pltpu.VMEM((PAIRS, 3, PAIR, PAIR), BF16),
            pltpu.VMEM((2, PAIR, width), F32),
            pltpu.VMEM((PAIRS, PAIR, width), BF16),
            pltpu.VMEM((2, PAIR, width), F32),
            pltpu.VMEM((2, PAIR, width), F32),
            pltpu.VMEM((2, PAIR, width), BF16),
            pltpu.VMEM((2, PAIR, width), BF16),
            pltpu.VMEM((2, PAIR, width), BF16),
            pltpu.VMEM((2, PAIR + 8, BLK), F32),
            pltpu.VMEM((8, width), F32),
            pltpu.VMEM((PAIR + 8, BLK), F32),
            pltpu.VMEM((PLANE, PIECE + 8, BLK), F32),
            pltpu.VMEM((PLANE, PIECE + 8, BLK), F32),
            pltpu.VMEM((4, PIECE + 8, BLK), F32),
            pltpu.VMEM((4, PIECE + 8, BLK), F32),
            pltpu.VMEM((PAIR + 8, BLK), F32),
            pltpu.VMEM((PAIR + 8, BLK), F32),
            sem((3,)), sem((2,)), sem((2,)), sem((2, PARTS)), sem((2, PARTS)),
            sem, sem, sem((PLANE,)), sem((PLANE,)), sem((3,)), sem((4,)), sem((3,)), sem((4,)),
            sem((PLANE,)), sem((PLANE,)), sem, sem,
        ],
        compiler_params=pltpu.CompilerParams(
            collective_id=0, has_side_effects=True, vmem_limit_bytes=56 << 20
        ),
        name="graph_layer",
    )(features, adj_values, adj_offset.T, adj_count, weight, bias_vector.reshape(1, width), cotangent)
    activated, grad_features, grad_weight, grad_bias = pl.pallas_call(
        write_out,
        out_shape=(
            jax.ShapeDtypeStruct((nodes, width), BF16),
            jax.ShapeDtypeStruct((nodes, width), BF16),
            jax.ShapeDtypeStruct((width, width), F32),
            jax.ShapeDtypeStruct((1, width), F32),
        ),
        in_specs=[vmem] * 4,
        out_specs=(anywhere,) * 4,
        scratch_shapes=[sem((4,))],
        name="write_out",
    )(*[pltpu.with_memory_space_constraint(r, pltpu.VMEM) for r in results])
    return activated, grad_features, grad_weight, grad_bias.reshape(width)


def solution(mesh):
    both = ("rows", "cols")
    return jax.shard_map(
        on_device,
        mesh=mesh,
        in_specs=(P(both, None), P(both, None, None, None), P(both, None), P(both), P(), P(), P(both, None)),
        out_specs=(P(both, None), P(both, None), P(), P()),
        check_vma=False,
    )
```

```python
import functools
import math

import jax
import jax.numpy as jnp
from jax import lax
from jax.experimental import pallas as pl
from jax.experimental.pallas import tpu as pltpu
from jax.sharding import PartitionSpec as P

MESH = pl.DeviceIdType.MESH
F32 = jnp.float32
BF16 = jnp.bfloat16
BLK = 128
PAIR = 256
PAIRS = 6
SLOTS = 3
PLANE = 16
PARTS = 4
PIECE = 16


def dot(a, b):
    return jnp.dot(a, b, preferred_element_type=F32)


def dot_t(a, b):
    return lax.dot_general(a, b, (((0,), (0,)), ((), ())), preferred_element_type=F32)


def place():
    rows, cols = lax.axis_index("rows"), lax.axis_index("cols")
    return rows // 16, cols // 2, (cols % 2) * 8 + (rows // 2) % 8, rows % 2


def device(x, y, z, core):
    return ((x * 8 + z % 8) * 2 + core, y * 2 + z // 8)


def along(step):
    flat = (lax.axis_index("rows") * 8 + lax.axis_index("cols") + step + 512) % 512
    return (flat // 8, flat % 8)


def kernel(
    norm_scale,
    feat_hbm, adj_hbm, off_ref, cnt_ref, w_ref, bias_ref, cot_hbm,
    act_ref, gf_ref, gw_ref, gb_ref,
    x_ref, a_ref, cot_ref, tile_ref, edge_acc, u_ref, gf_acc, gf_edge,
    halo, spill, landed, grad_half, bias_acc,
    from_core, plane_out, plane_in, z_near, z_far, full_half, other_half,
    load_sem, halo_send, halo_recv, spill_send, spill_recv,
    core_send, core_recv, plane_send, plane_recv, near_send, near_recv, far_send, far_recv,
    gather_send, gather_recv, back_send, back_recv,
):
    x, y, z, core = place()
    mine = x * 4 + y
    group, member = z // 4, z % 4

    def plane_peer(step):
        j = (mine + step) % PLANE
        return j, device(j // 4, j % 4, z, core)

    def near_peer(step):
        m = (member + step) % 4
        return device(x, y, group * 4 + m, core)

    def far_peer(step):
        g = (group + step) % 4
        return device(x, y, g * 4 + member, core)

    other_core = device(x, y, z, 1 - core)

    entry = pltpu.get_barrier_semaphore()

    def greet(target):
        pl.semaphore_signal(entry, inc=1, device_id=target, device_id_type=MESH)

    greet(along(1))
    greet(along(-1))
    for step in range(1, 4):
        greet(far_peer(step))
    for step in range(1, PLANE):
        greet(plane_peer(step)[1])
    for step in range(1, 4):
        greet(near_peer(step))
    greet(other_core)

    loads = [
        pltpu.make_async_copy(adj_hbm, a_ref.at[pl.ds(0, 2 * PAIRS)], load_sem.at[0]),
        pltpu.make_async_copy(feat_hbm, x_ref, load_sem.at[1]),
        pltpu.make_async_copy(cot_hbm, cot_ref, load_sem.at[2]),
    ]
    for load in loads:
        load.start()
    for s in range(SLOTS):
        a_ref[2 * PAIRS, s] = jnp.zeros((BLK, BLK), BF16)
    bias_acc[...] = jnp.zeros_like(bias_acc)
    grad_half[...] = jnp.zeros_like(grad_half)
    loads[0].wait()

    def build(p, carry):
        for r in range(2):
            i = 2 * p + r
            count = cnt_ref[i]
            offs = [off_ref[s, i] for s in range(SLOTS)]
            for q in range(3):
                for c in range(2):
                    k = 2 * (q - 1) + c - r
                    at = (pl.ds(r * BLK, BLK), pl.ds(c * BLK, BLK))
                    if abs(k) > 2:
                        tile_ref[p, q, at[0], at[1]] = jnp.zeros((BLK, BLK), BF16)
                        continue
                    row, slot = jnp.int32(2 * PAIRS), jnp.int32(0)
                    for s in range(SLOTS):
                        hit = jnp.logical_and(offs[s] == k, s < count)
                        row = jnp.where(hit, i, row)
                        slot = jnp.where(hit, s, slot)
                    tile_ref[p, q, at[0], at[1]] = a_ref[row, slot]
        return carry

    lax.fori_loop(0, PAIRS, build, 0)
    loads[1].wait()
    loads[2].wait()

    def layer(p, summed):
        rows = pl.ds(pl.multiple_of(p * PAIR, PAIR), PAIR)
        agg = summed.astype(BF16)
        pre = dot(agg, w_ref[...]) + bias_ref[...]
        q = jax.nn.sigmoid(pre)
        act_ref[rows, :] = (pre * q).astype(BF16)
        grad_pre = (cot_ref[rows, :].astype(F32) * q * (1.0 + pre * (1.0 - q))).astype(BF16)
        up = lax.dot_general(
            grad_pre, w_ref[...], (((1,), (1,)), ((), ())), preferred_element_type=F32
        ).astype(BF16)
        u_ref[p] = up
        gw = dot_t(agg, grad_pre)
        grad_half[0, pl.ds(0, PAIR)] += gw[:, :BLK]
        grad_half[1, pl.ds(0, PAIR)] += gw[:, BLK:]
        bias_acc[...] += jnp.sum(grad_pre.astype(F32).reshape(PAIR // 8, 8, PAIR), axis=0)

    def x_pair(p):
        return x_ref[pl.ds(pl.multiple_of(p * PAIR, PAIR), PAIR), :]

    def forward(p, carry):
        layer(
            p,
            dot(tile_ref[p, 0], x_pair(p - 1))
            + dot(tile_ref[p, 1], x_pair(p))
            + dot(tile_ref[p, 2], x_pair(p + 1)),
        )
        return carry

    lax.fori_loop(1, PAIRS - 1, forward, 0)

    pl.semaphore_wait(entry, 2 + 3 + 15 + 3 + 1)

    def rim(side):
        return pltpu.make_async_remote_copy(
            src_ref=x_ref.at[pl.ds((1 - side) * (PAIRS - 1) * PAIR, PAIR)],
            dst_ref=halo.at[side],
            send_sem=halo_send.at[side],
            recv_sem=halo_recv.at[side],
            device_id=along(1 - 2 * side),
            device_id_type=MESH,
        )

    rim(0).start()
    rim(1).start()

    def edge_start(side, carry):
        p = side * (PAIRS - 1)
        edge_acc[side] = dot(tile_ref[p, 1], x_pair(p)) + dot(
            tile_ref[p, 2 - 2 * side], x_pair(1 + 3 * side)
        )
        return carry

    lax.fori_loop(0, 2, edge_start, 0)

    def inner(side, carry):
        near = 1 + 3 * side
        deep = 2 + side
        gf_acc[side] = dot_t(tile_ref[near, 1], u_ref[near]) + dot_t(
            tile_ref[deep, 2 * side], u_ref[deep]
        )
        gf_edge[side] = dot_t(tile_ref[near, 2 * side], u_ref[near])
        total = (
            dot_t(tile_ref[deep - 1, 2], u_ref[deep - 1])
            + dot_t(tile_ref[deep, 1], u_ref[deep])
            + dot_t(tile_ref[deep + 1, 0], u_ref[deep + 1])
        )
        gf_ref[pl.ds(pl.multiple_of(deep * PAIR, PAIR), PAIR), :] = total.astype(BF16)
        return carry

    lax.fori_loop(0, 2, inner, 0)

    def back_copy(side, part):
        rows = pl.ds(part * (PAIR // PARTS), PAIR // PARTS)
        return pltpu.make_async_remote_copy(
            src_ref=spill.at[side, rows],
            dst_ref=landed.at[1 - side, rows],
            send_sem=spill_send.at[side, part],
            recv_sem=spill_recv.at[1 - side, part],
            device_id=along(2 * side - 1),
            device_id_type=MESH,
        )

    def edge_layer(side):
        p = side * (PAIRS - 1)
        rim(side).wait_recv()
        layer(p, edge_acc[side] + dot(tile_ref[p, 2 * side], halo[side]))

    def edge_back(side):
        p = side * (PAIRS - 1)
        up = u_ref[p]
        spill[side] = dot_t(tile_ref[p, 2 * side], up).astype(BF16)
        near = 1 + 3 * side
        gf_ref[pl.ds(near * PAIR, PAIR), :] = (
            gf_acc[side] + dot_t(tile_ref[p, 2 - 2 * side], up)
        ).astype(BF16)
        gf_edge[side] += dot_t(tile_ref[p, 1], up)

    edge_layer(0)
    edge_back(0)
    edge_layer(1)

    grad_half[0, pl.ds(PAIR, 8)] = bias_acc[:, :BLK]
    grad_half[1, pl.ds(PAIR, 8)] = bias_acc[:, BLK:]
    to_core = pltpu.make_async_remote_copy(
        src_ref=grad_half.at[1 - core], dst_ref=from_core, send_sem=core_send, recv_sem=core_recv,
        device_id=other_core, device_id_type=MESH,
    )
    to_core.start()
    edge_back(1)
    back_copy(0, 0).start()
    back_copy(1, 0).start()
    to_core.wait()
    bias_rows = grad_half[core, pl.ds(PAIR, 8)] + from_core[pl.ds(PAIR, 8)]
    for j in range(PLANE):
        rows = pl.ds(j * PIECE, PIECE)
        plane_out[j, pl.ds(0, PIECE)] = grad_half[core, rows] + from_core[rows]
        plane_out[j, pl.ds(PIECE, 8)] = bias_rows

    def plane_copy(step):
        j, target = plane_peer(step)
        return pltpu.make_async_remote_copy(
            src_ref=plane_out.at[j], dst_ref=plane_in.at[mine],
            send_sem=plane_send.at[j], recv_sem=plane_recv.at[mine],
            device_id=target, device_id_type=MESH,
        )

    def plane_arrival(step):
        j, target = plane_peer(step)
        return pltpu.make_async_remote_copy(
            src_ref=plane_out.at[j], dst_ref=plane_in.at[j],
            send_sem=plane_send.at[j], recv_sem=plane_recv.at[j],
            device_id=target, device_id_type=MESH,
        )

    for step in range(1, PLANE):
        plane_copy(step).start()
    plane_in[mine] = plane_out[mine]
    for step in range(1, PLANE):
        plane_arrival(step).wait()
    total = plane_in[0]
    for j in range(1, PLANE):
        total = total + plane_in[j]

    z_near[member] = total

    def near_copy(step):
        return pltpu.make_async_remote_copy(
            src_ref=z_near.at[member], dst_ref=z_near.at[member],
            send_sem=near_send.at[step - 1], recv_sem=near_recv.at[member],
            device_id=near_peer(step), device_id_type=MESH,
        )

    def near_arrival(step):
        m = (member + step) % 4
        return pltpu.make_async_remote_copy(
            src_ref=z_near.at[m], dst_ref=z_near.at[m],
            send_sem=near_send.at[step - 1], recv_sem=near_recv.at[m],
            device_id=near_peer(step), device_id_type=MESH,
        )

    for step in range(1, 4):
        near_copy(step).start()
    back_copy(0, 1).start()
    back_copy(1, 1).start()
    for step in range(1, 4):
        near_arrival(step).wait()
    z_far[group] = (z_near[0] + z_near[1]) + (z_near[2] + z_near[3])

    def far_copy(step):
        return pltpu.make_async_remote_copy(
            src_ref=z_far.at[group], dst_ref=z_far.at[group],
            send_sem=far_send.at[step - 1], recv_sem=far_recv.at[group],
            device_id=far_peer(step), device_id_type=MESH,
        )

    def far_arrival(step):
        g = (group + step) % 4
        return pltpu.make_async_remote_copy(
            src_ref=z_far.at[g], dst_ref=z_far.at[g],
            send_sem=far_send.at[step - 1], recv_sem=far_recv.at[g],
            device_id=far_peer(step), device_id_type=MESH,
        )

    for step in range(1, 4):
        far_copy(step).start()
    back_copy(0, 2).start()
    back_copy(0, 3).start()
    back_copy(1, 2).start()
    back_copy(1, 3).start()

    def finish(side):
        for part in range(PARTS):
            back_copy(1 - side, part).wait_recv()
        rows = pl.ds(side * (PAIRS - 1) * PAIR, PAIR)
        gf_ref[rows, :] = (gf_edge[side] + landed[side].astype(F32)).astype(BF16)

    for step in range(1, 4):
        far_arrival(step).wait()
    total = ((z_far[0] + z_far[1]) + (z_far[2] + z_far[3])) * norm_scale
    full_half[pl.ds(pl.multiple_of(mine * PIECE, PIECE), PIECE), :] = total[:PIECE]
    full_half[pl.ds(PAIR, 8), :] = jnp.broadcast_to(jnp.sum(total[PIECE:], axis=0, keepdims=True), (8, BLK))

    def piece(j):
        return full_half.at[pl.ds(pl.multiple_of(j * PIECE, PIECE), PIECE)]

    def gather_copy(step):
        j, target = plane_peer(step)
        return pltpu.make_async_remote_copy(
            src_ref=piece(mine), dst_ref=piece(mine),
            send_sem=gather_send.at[j], recv_sem=gather_recv.at[mine],
            device_id=target, device_id_type=MESH,
        )

    def gather_arrival(step):
        j, target = plane_peer(step)
        return pltpu.make_async_remote_copy(
            src_ref=piece(j), dst_ref=piece(j),
            send_sem=gather_send.at[j], recv_sem=gather_recv.at[j],
            device_id=target, device_id_type=MESH,
        )

    for step in range(1, PLANE):
        gather_copy(step).start()
    for step in range(1, PLANE):
        gather_arrival(step).wait()
    across = pltpu.make_async_remote_copy(
        src_ref=full_half, dst_ref=other_half, send_sem=back_send, recv_sem=back_recv,
        device_id=other_core, device_id_type=MESH,
    )
    across.start()
    across.wait()
    low = jnp.where(core == 0, full_half[...], other_half[...])
    high = jnp.where(core == 0, other_half[...], full_half[...])
    gw_ref[:, :BLK] = low[:PAIR]
    gw_ref[:, BLK:] = high[:PAIR]
    gb_ref[:, :BLK] = low[PAIR : PAIR + 1]
    gb_ref[:, BLK:] = high[PAIR : PAIR + 1]
    finish(1)
    finish(0)
    rim(0).wait_send()
    rim(1).wait_send()
    for side in range(2):
        for part in range(PARTS):
            back_copy(side, part).wait_send()


def write_out(*refs):
    sems = refs[-1]
    copies = [pltpu.make_async_copy(refs[k], refs[4 + k], sems.at[k]) for k in range(4)]
    for copy in copies:
        copy.start()
    for copy in copies:
        copy.wait()


def on_device(features, adj_values, adj_offset, adj_count, weight, bias_vector, cotangent):
    nodes, width = features.shape
    nodes_total = nodes * lax.axis_size("rows") * lax.axis_size("cols")
    vmem = pl.BlockSpec(memory_space=pltpu.VMEM)
    smem = pl.BlockSpec(memory_space=pltpu.SMEM)
    anywhere = pl.BlockSpec(memory_space=pl.ANY)
    sem = pltpu.SemaphoreType.DMA
    results = pl.pallas_call(
        functools.partial(kernel, 1.0 / math.sqrt(nodes_total)),
        out_shape=(
            pltpu.VMEM((nodes, width), BF16),
            pltpu.VMEM((nodes, width), BF16),
            pltpu.VMEM((width, width), F32),
            pltpu.VMEM((1, width), F32),
        ),
        in_specs=[anywhere, anywhere, smem, smem, vmem, vmem, anywhere],
        out_specs=(vmem, vmem, vmem, vmem),
        scratch_shapes=[
            pltpu.VMEM((nodes, width), BF16),
            pltpu.VMEM((2 * PAIRS + 1, SLOTS, BLK, BLK), BF16),
            pltpu.VMEM((nodes, width), BF16),
            pltpu.VMEM((PAIRS, 3, PAIR, PAIR), BF16),
            pltpu.VMEM((2, PAIR, width), F32),
            pltpu.VMEM((PAIRS, PAIR, width), BF16),
            pltpu.VMEM((2, PAIR, width), F32),
            pltpu.VMEM((2, PAIR, width), F32),
            pltpu.VMEM((2, PAIR, width), BF16),
            pltpu.VMEM((2, PAIR, width), BF16),
            pltpu.VMEM((2, PAIR, width), BF16),
            pltpu.VMEM((2, PAIR + 8, BLK), F32),
            pltpu.VMEM((8, width), F32),
            pltpu.VMEM((PAIR + 8, BLK), F32),
            pltpu.VMEM((PLANE, PIECE + 8, BLK), F32),
            pltpu.VMEM((PLANE, PIECE + 8, BLK), F32),
            pltpu.VMEM((4, PIECE + 8, BLK), F32),
            pltpu.VMEM((4, PIECE + 8, BLK), F32),
            pltpu.VMEM((PAIR + 8, BLK), F32),
            pltpu.VMEM((PAIR + 8, BLK), F32),
            sem((3,)), sem((2,)), sem((2,)), sem((2, PARTS)), sem((2, PARTS)),
            sem, sem, sem((PLANE,)), sem((PLANE,)), sem((3,)), sem((4,)), sem((3,)), sem((4,)),
            sem((PLANE,)), sem((PLANE,)), sem, sem,
        ],
        compiler_params=pltpu.CompilerParams(
            collective_id=0, has_side_effects=True, vmem_limit_bytes=56 << 20
        ),
        name="graph_layer",
    )(features, adj_values, adj_offset.T, adj_count, weight, bias_vector.reshape(1, width), cotangent)
    activated, grad_features, grad_weight, grad_bias = pl.pallas_call(
        write_out,
        out_shape=(
            jax.ShapeDtypeStruct((nodes, width), BF16),
            jax.ShapeDtypeStruct((nodes, width), BF16),
            jax.ShapeDtypeStruct((width, width), F32),
            jax.ShapeDtypeStruct((1, width), F32),
        ),
        in_specs=[vmem] * 4,
        out_specs=(anywhere,) * 4,
        scratch_shapes=[sem((4,))],
        name="write_out",
    )(*[pltpu.with_memory_space_constraint(r, pltpu.VMEM) for r in results])
    return activated, grad_features, grad_weight, grad_bias.reshape(width)


def solution(mesh):
    both = ("rows", "cols")
    return jax.shard_map(
        on_device,
        mesh=mesh,
        in_specs=(P(both, None), P(both, None, None, None), P(both, None), P(both), P(), P(), P(both, None)),
        out_specs=(P(both, None), P(both, None), P(), P()),
        check_vma=False,
    )
```
